32 devices in a mesh: long: 8 (over z, core), grp: 4 (over y, x).
Axes of the slice: x: 2, y: 2, z: 4, core: 2. Of those that a mesh axis runs over, the one named last changes fastest.
Arguments:
- amplitudes: bfloat16 [8192, 12288], P('long', 'grp'), may hold values from -6 to 6
- integrals: bfloat16 [12288, 4096], P('grp', 'long'), may hold values from -0.078125 to 0.078125
- amp_pattern: int32 [128, 192], P('long', 'grp'), may hold values 0 or 1
- int_pattern: int32 [192, 64], P('grp', 'long'), may hold values 0 or 1
- owners: int32 [4], replicated, may hold values from 0 to 7
Outputs:
- ladder: bfloat16 [4, 1024, 4096], P(None, None, ('long', 'grp'))
The draws below stay inside these ranges and needn't reach their ends.
Inputs may be any that keep to these rules, and one draw needn't show every extreme that they name: `amp_pattern`: tile present (1) or absent (0). `int_pattern`: tile present (1) or absent (0).
All inputs are finite; a program needn't handle non-finite values. No bound on the sum of `amp_pattern` or of `int_pattern` on one device may be relied on, other than what follows from the above.
Results may differ from the reference program's by a relative error of at most 0.001.
Values may be sent and summed in bfloat16 or wider, within the bound.
A program may use at most 192 MiB of HBM per device.

```python
import jax
import jax.numpy as jnp
from jax import lax

TILE = 64
PR = 1024
STEPS = 4
ROWS = 8192
KCOLS = 12288
NCOLS = 4096
N_LONG = 8


def plant(values, stream_key, smallest, largest):
    longest = values.shape.index(max(values.shape))
    spots = []
    for shift in (0, 1):
        where = [jax.random.randint(jax.random.fold_in(stream_key, axis), (), 0, length) for axis, length in enumerate(values.shape)]
        where[longest] = (where[longest] + shift) % values.shape[longest]
        spots.append(tuple(where))
    return values.at[spots[0]].set(smallest).at[spots[1]].set(largest)


def shard_levels(key, extent, cuts, smallest, high):
    def one(axis_at, parts):
        draws = jax.random.uniform(jax.random.fold_in(jax.random.fold_in(key, 6), axis_at), (parts,), jnp.float32, smallest / len(cuts), high / len(cuts))
        return jnp.repeat(jnp.exp(draws), extent[axis_at] // parts).reshape((-1,) + (1,) * (len(extent) - axis_at - 1))

    level = one(*cuts[0])
    for cut in cuts[1:]:
        level = level * one(*cut)
    return level


def scatter_about(rng, shape, spread, reach, split=(), held_as=jnp.bfloat16):
    values = jax.random.normal(rng, shape, jnp.float32) * spread
    if len(split) > 0:
        values = shard_levels(rng, shape, split, -0.22, 0.18) * values
    return jnp.clip(values, min=-reach, max=reach).astype(held_as)


def setup_inputs(seed: int = 0) -> dict:
    keys = jax.random.split(jax.random.key(seed), 6)
    amplitudes = scatter_about(keys[0], (ROWS, KCOLS), 1.0, 6.0, ((0, 8), (1, 4)))
    integrals = scatter_about(keys[1], (KCOLS, NCOLS), (KCOLS // 2) ** -0.5, 0.078125, ((0, 4), (1, 8)))
    amp_pattern = plant((jax.random.randint(keys[2], (ROWS // TILE, KCOLS // TILE), 0, 2) < 1).astype(jnp.int32), jax.random.fold_in(keys[2], 1), 0, 1)
    int_pattern = plant((jax.random.randint(keys[3], (KCOLS // TILE, NCOLS // TILE), 0, 2) < 1).astype(jnp.int32), jax.random.fold_in(keys[3], 1), 0, 1)
    owners = plant(jax.random.randint(keys[4], (STEPS,), 0, N_LONG), jax.random.fold_in(keys[4], 1), 0, N_LONG - 1).astype(jnp.int32)
    return {"amplitudes": amplitudes, "integrals": integrals, "amp_pattern": amp_pattern, "int_pattern": int_pattern, "owners": owners}


def spread_mask(values, pattern):
    row_tiles, col_tiles = pattern.shape
    shaped = values.reshape(row_tiles, TILE, col_tiles, TILE)
    scaled = shaped * pattern.astype(values.dtype)[:, None, :, None]
    return scaled.reshape(row_tiles * TILE, col_tiles * TILE)


def reference(amplitudes, integrals, amp_pattern, int_pattern, owners):
    sparse_amp = spread_mask(amplitudes, amp_pattern)
    sparse_int = spread_mask(integrals, int_pattern)
    results = []
    for step in range(STEPS):
        start = (owners[step] * PR).astype(jnp.int32)
        rows_block = lax.dynamic_slice_in_dim(sparse_amp, start, PR, 0)
        results.append(jnp.dot(rows_block, sparse_int, preferred_element_type=jnp.float32).astype(jnp.bfloat16))
    return jnp.stack(results, 0)
```

```python
import functools

import jax
import jax.numpy as jnp
from jax import lax
from jax.experimental import pallas as pl
from jax.experimental.pallas import tpu as pltpu
from jax.sharding import PartitionSpec as P

TILE = 64
LANES = 128
CHUNKS = 4
SHARE = (3, 5)
BLOCK = 256


def broadcast(shard, axis, root):
    mine = lax.axis_index(axis) == root
    return lax.psum(jnp.where(mine, shard, jnp.zeros_like(shard)), axis)


def spread(pattern, dtype):
    row_tiles, col_tiles = pattern.shape
    down = jnp.arange(row_tiles * TILE)[:, None] // TILE == jnp.arange(row_tiles)[None, :]
    across = jnp.arange(col_tiles * TILE)[None, :] // TILE == jnp.arange(col_tiles)[:, None]
    rows = jnp.dot(down.astype(dtype), pattern.astype(dtype), preferred_element_type=dtype)
    return jnp.dot(rows, across.astype(dtype), preferred_element_type=dtype)


def dense_path(amplitudes, sparse_int, amp_pattern, owners):
    sparse_amp = amplitudes * spread(amp_pattern, amplitudes.dtype)

    def step(_, owner):
        panel = broadcast(sparse_amp, "long", owner)
        partial_value = jnp.dot(panel, sparse_int, preferred_element_type=jnp.float32)
        total = lax.psum_scatter(partial_value, "grp", scatter_dimension=1, tiled=True)
        return None, total.astype(amplitudes.dtype)

    return lax.scan(step, None, owners)[1]


def halves(dtype):
    lane = lax.broadcasted_iota(jnp.int32, (TILE, LANES), 1)
    left = (lane < TILE).astype(jnp.float32).astype(dtype)
    right = (lane >= TILE).astype(jnp.float32).astype(dtype)
    return left, right


def pack_kernel(where_ref, a_ref, out_ref):
    left, right = halves(out_ref.dtype)

    def tile(slot, parity):
        row = pl.multiple_of(where_ref[2 * parity, slot], TILE)
        col = pl.multiple_of(where_ref[2 * parity + 1, slot], LANES)
        return a_ref[pl.ds(row, TILE), pl.ds(col, LANES)]

    def body(slot, _):
        to = pl.multiple_of(slot * TILE, TILE)
        out_ref[pl.ds(to, TILE), :] = tile(slot, 0) * left + tile(slot, 1) * right
        return 0

    lax.fori_loop(0, out_ref.shape[0] // TILE, body, 0, unroll=4)


def pack(amplitudes, spots, slots):
    return pl.pallas_call(
        pack_kernel,
        out_shape=jax.ShapeDtypeStruct((slots * TILE, LANES), amplitudes.dtype),
        grid_spec=pltpu.PrefetchScalarGridSpec(
            num_scalar_prefetch=1,
            grid=(1,),
            in_specs=[pl.BlockSpec(amplitudes.shape, lambda i, w: (0, 0))],
            out_specs=pl.BlockSpec((slots * TILE, LANES), lambda i, w: (0, 0)),
        ),
    )(spots, amplitudes)


def multiply_kernel(pairs, rank_ref, packed_ref, b_ref, out_ref, dense_ref):
    left, right = halves(dense_ref.dtype)
    row_tiles = dense_ref.shape[0] // TILE
    first = pl.program_id(0) * row_tiles * pairs

    def body(row, _):
        to = pl.multiple_of(row * TILE, TILE)
        for col in range(pairs):
            at = first + row * pairs + col
            even = pl.multiple_of(rank_ref[0, at], TILE)
            odd = pl.multiple_of(rank_ref[1, at], TILE)
            dense_ref[pl.ds(to, TILE), col * LANES : (col + 1) * LANES] = (
                packed_ref[pl.ds(even, TILE), :] * left + packed_ref[pl.ds(odd, TILE), :] * right
            )
        return 0

    lax.fori_loop(0, row_tiles, body, 0)
    out_ref[...] = jnp.dot(dense_ref[...], b_ref[...], preferred_element_type=jnp.float32)


def multiply(packed, ranks, b, rows):
    depth, cols = b.shape
    block = min(BLOCK, rows)
    return pl.pallas_call(
        functools.partial(multiply_kernel, depth // LANES),
        out_shape=jax.ShapeDtypeStruct((rows, cols), jnp.float32),
        grid_spec=pltpu.PrefetchScalarGridSpec(
            num_scalar_prefetch=1,
            grid=(rows // block,),
            in_specs=[
                pl.BlockSpec(packed.shape, lambda i, r: (0, 0)),
                pl.BlockSpec(b.shape, lambda i, r: (0, 0)),
            ],
            out_specs=pl.BlockSpec((block, cols), lambda i, r: (i, 0)),
            scratch_shapes=[pltpu.VMEM((block, depth), packed.dtype)],
        ),
        cost_estimate=pl.CostEstimate(
            flops=2 * rows * depth * cols,
            bytes_accessed=packed.size * 2 + b.size * 2 + rows * cols * 4,
            transcendentals=0,
        ),
    )(ranks, packed, b)


def by_parity(pattern):
    *lead, row_tiles, col_tiles = pattern.shape
    flat = pattern.reshape(*lead, row_tiles * col_tiles // 2, 2)
    flat = jnp.swapaxes(flat, -1, -2)
    return flat, jnp.cumsum(flat, axis=-1)


def per_device(long, grp, amplitudes, integrals, amp_pattern, int_pattern, owners):
    steps = owners.shape[0]
    chips = long // 2
    rows, depth = amplitudes.shape
    pairs = depth // LANES
    slots = -(-(rows // TILE) * pairs * SHARE[0] // (SHARE[1] * 2 * CHUNKS)) * 2 * CHUNKS
    half = slots // 2 * TILE
    piece = half // CHUNKS

    me = lax.axis_index("long")
    chip, core = me // 2, me % 2
    swap = [(i, i ^ 1) for i in range(long)]
    up = [(i, i + 2) for i in range(long - 2)]
    down = [(i + 2, i) for i in range(long - 2)]

    _, count = by_parity(amp_pattern)
    spot = jnp.sum(count[:, None, :] <= jnp.arange(slots)[None, :, None], axis=-1)
    spot = jnp.minimum(spot, count.shape[-1] - 1)
    spots = jnp.stack([spot // pairs * TILE, spot % pairs * LANES], 1).reshape(4, slots)
    packed = pack(amplitudes, spots.astype(jnp.int32), slots)

    patterns = lax.all_gather(amp_pattern, ("long", "grp"))
    patterns = patterns.reshape(long, grp, *amp_pattern.shape)[owners]
    full = jnp.any(jnp.sum(by_parity(patterns)[0], axis=-1) > slots)
    here, count = by_parity(lax.dynamic_index_in_dim(patterns, lax.axis_index("grp"), 1, False))
    rank = (count - 1 + core * (slots // 2)) % slots
    ranks = jnp.where(here > 0, jnp.minimum(rank, slots), slots).astype(jnp.int32) * TILE

    sparse_int = integrals * spread(int_pattern, integrals.dtype)

    keep = lax.dynamic_slice_in_dim(packed, core * half, half, 0)
    give = lax.dynamic_slice_in_dim(packed, (1 - core) * half, half, 0)
    gain = lax.ppermute(give, "long", swap)

    def own(number):
        at = number % CHUNKS * piece
        mine = owners[number // CHUNKS] % 2 == core
        return jnp.where(
            mine,
            lax.dynamic_slice_in_dim(keep, at, piece, 0),
            lax.dynamic_slice_in_dim(gain, at, piece, 0),
        )

    pieces = steps * CHUNKS

    def outgoing(number, carried):
        number = jnp.clip(number, 0, pieces - 1)
        mine = owners[number // CHUNKS] // 2 == chip
        return own(number) if carried is None else jnp.where(mine, own(number), carried)

    rose, fell = [], []
    for turn in range(pieces + chips - 2):
        rising = outgoing(turn - chip, rose[-1] if rose else None)
        falling = outgoing(turn - (chips - 1 - chip), fell[-1] if fell else None)
        rose.append(lax.ppermute(rising, "long", up))
        fell.append(lax.ppermute(falling, "long", down))

    results = []
    for step in range(steps):
        source = owners[step] // 2
        kept = []
        for number in range(step * CHUNKS, (step + 1) * CHUNKS):
            value = own(number)
            for place in range(chips):
                if place > 0:
                    below = (chip == place) & (source < chip)
                    value = jnp.where(below, rose[number + place - 1], value)
                if place < chips - 1:
                    above = (chip == place) & (source > chip)
                    value = jnp.where(above, fell[number + chips - 2 - place], value)
            kept.append(value)
        other = [lax.ppermute(value, "long", swap) for value in kept]
        nothing = jnp.zeros((TILE, LANES), amplitudes.dtype)
        panel = jnp.concatenate(kept + other + [nothing], 0)
        partial_value = multiply(panel, ranks[step], sparse_int, rows)
        total = lax.psum_scatter(partial_value, "grp", scatter_dimension=1, tiled=True)
        results.append(total.astype(amplitudes.dtype))
    quick = jnp.stack(results, 0)

    return lax.cond(
        full,
        lambda: dense_path(amplitudes, sparse_int, amp_pattern, owners),
        lambda: quick,
    )


def solution(mesh):
    placed = (P("long", "grp"), P("grp", "long"), P("long", "grp"), P("grp", "long"), P())
    return jax.shard_map(
        functools.partial(per_device, mesh.shape["long"], mesh.shape["grp"]),
        mesh=mesh,
        in_specs=placed,
        out_specs=P(None, None, ("long", "grp")),
        check_vma=False,
    )
```

```python
import functools

import jax
import jax.numpy as jnp
from jax import lax
from jax.experimental import pallas as pl
from jax.experimental.pallas import tpu as pltpu
from jax.sharding import PartitionSpec as P

TILE = 64
LANES = 128
CHUNKS = 2
SHARE = (3, 5)
BLOCK = 256


def broadcast(shard, axis, root):
    mine = lax.axis_index(axis) == root
    return lax.psum(jnp.where(mine, shard, jnp.zeros_like(shard)), axis)


def spread(pattern, dtype):
    row_tiles, col_tiles = pattern.shape
    down = jnp.arange(row_tiles * TILE)[:, None] // TILE == jnp.arange(row_tiles)[None, :]
    across = jnp.arange(col_tiles * TILE)[None, :] // TILE == jnp.arange(col_tiles)[:, None]
    rows = jnp.dot(down.astype(dtype), pattern.astype(dtype), preferred_element_type=dtype)
    return jnp.dot(rows, across.astype(dtype), preferred_element_type=dtype)


def dense_path(amplitudes, sparse_int, amp_pattern, owners):
    sparse_amp = amplitudes * spread(amp_pattern, amplitudes.dtype)

    def step(_, owner):
        panel = broadcast(sparse_amp, "long", owner)
        partial_value = jnp.dot(panel, sparse_int, preferred_element_type=jnp.float32)
        total = lax.psum_scatter(partial_value, "grp", scatter_dimension=1, tiled=True)
        return None, total.astype(amplitudes.dtype)

    return lax.scan(step, None, owners)[1]


def halves(dtype):
    lane = lax.broadcasted_iota(jnp.int32, (TILE, LANES), 1)
    left = (lane < TILE).astype(jnp.float32).astype(dtype)
    right = (lane >= TILE).astype(jnp.float32).astype(dtype)
    return left, right


def pack_kernel(where_ref, a_ref, out_ref):
    left, right = halves(out_ref.dtype)

    def tile(slot, parity):
        row = pl.multiple_of(where_ref[2 * parity, slot], TILE)
        col = pl.multiple_of(where_ref[2 * parity + 1, slot], LANES)
        return a_ref[pl.ds(row, TILE), pl.ds(col, LANES)]

    def body(slot, _):
        to = pl.multiple_of(slot * TILE, TILE)
        out_ref[pl.ds(to, TILE), :] = tile(slot, 0) * left + tile(slot, 1) * right
        return 0

    lax.fori_loop(0, out_ref.shape[0] // TILE, body, 0, unroll=4)


def pack(amplitudes, spots, slots):
    return pl.pallas_call(
        pack_kernel,
        out_shape=jax.ShapeDtypeStruct((slots * TILE, LANES), amplitudes.dtype),
        grid_spec=pltpu.PrefetchScalarGridSpec(
            num_scalar_prefetch=1,
            grid=(1,),
            in_specs=[pl.BlockSpec(amplitudes.shape, lambda i, w: (0, 0))],
            out_specs=pl.BlockSpec((slots * TILE, LANES), lambda i, w: (0, 0)),
        ),
    )(spots, amplitudes)


def multiply_kernel(pairs, rank_ref, packed_ref, b_ref, out_ref, dense_ref):
    left, right = halves(dense_ref.dtype)
    row_tiles = dense_ref.shape[0] // TILE
    first = pl.program_id(0) * row_tiles * pairs

    def body(row, _):
        to = pl.multiple_of(row * TILE, TILE)
        for col in range(pairs):
            at = first + row * pairs + col
            even = pl.multiple_of(rank_ref[0, at], 16)
            odd = pl.multiple_of(rank_ref[1, at], 16)
            dense_ref[pl.ds(to, TILE), col * LANES : (col + 1) * LANES] = (
                packed_ref[pl.ds(even, TILE), :] * left + packed_ref[pl.ds(odd, TILE), :] * right
            )
        return 0

    lax.fori_loop(0, row_tiles, body, 0)
    out_ref[...] = jnp.dot(dense_ref[...], b_ref[...], preferred_element_type=jnp.float32)


def multiply(packed, ranks, b, rows):
    depth, cols = b.shape
    block = min(BLOCK, rows)
    return pl.pallas_call(
        functools.partial(multiply_kernel, depth // LANES),
        out_shape=jax.ShapeDtypeStruct((rows, cols), jnp.float32),
        grid_spec=pltpu.PrefetchScalarGridSpec(
            num_scalar_prefetch=1,
            grid=(rows // block,),
            in_specs=[
                pl.BlockSpec(packed.shape, lambda i, r: (0, 0)),
                pl.BlockSpec(b.shape, lambda i, r: (0, 0)),
            ],
            out_specs=pl.BlockSpec((block, cols), lambda i, r: (i, 0)),
            scratch_shapes=[pltpu.VMEM((block, depth), packed.dtype)],
        ),
        cost_estimate=pl.CostEstimate(
            flops=2 * rows * depth * cols,
            bytes_accessed=packed.size * 2 + b.size * 2 + rows * cols * 4,
            transcendentals=0,
        ),
    )(ranks, packed, b)


def by_parity(pattern):
    *lead, row_tiles, col_tiles = pattern.shape
    flat = pattern.reshape(*lead, row_tiles * col_tiles // 2, 2)
    flat = jnp.swapaxes(flat, -1, -2)
    return flat, jnp.cumsum(flat, axis=-1)


def per_device(long, grp, amplitudes, integrals, amp_pattern, int_pattern, owners):
    steps = owners.shape[0]
    chips = long // 2
    rows, depth = amplitudes.shape
    pairs = depth // LANES
    slots = -(-(rows // TILE) * pairs * SHARE[0] // (SHARE[1] * 2 * CHUNKS)) * 2 * CHUNKS
    half = slots // 2 * TILE
    note = -(-amp_pattern.shape[0] // 16) * 16
    piece = half // CHUNKS + note
    share = piece * CHUNKS

    me = lax.axis_index("long")
    chip, core = me // 2, me % 2
    swap = [(i, i ^ 1) for i in range(long)]
    up = [(i, i + 2) for i in range(long - 2)]
    down = [(i + 2, i) for i in range(long - 2)]

    _, count = by_parity(amp_pattern)
    spot = jnp.sum(count[:, None, :] <= jnp.arange(slots)[None, :, None], axis=-1)
    spot = jnp.minimum(spot, count.shape[-1] - 1)
    spots = jnp.stack([spot // pairs * TILE, spot % pairs * LANES], 1).reshape(4, slots)
    packed = pack(amplitudes, spots.astype(jnp.int32), slots)

    sparse_int = integrals * spread(int_pattern, integrals.dtype)

    tail = amp_pattern.astype(amplitudes.dtype)
    tail = jnp.pad(tail, ((0, share - half - tail.shape[0]), (0, LANES - tail.shape[1])))
    keep = jnp.concatenate([lax.dynamic_slice_in_dim(packed, core * half, half, 0), tail], 0)
    give = jnp.concatenate([lax.dynamic_slice_in_dim(packed, (1 - core) * half, half, 0), tail], 0)
    gain = lax.ppermute(give, "long", swap)

    def own(number):
        at = number % CHUNKS * piece
        mine = owners[number // CHUNKS] % 2 == core
        return jnp.where(
            mine,
            lax.dynamic_slice_in_dim(keep, at, piece, 0),
            lax.dynamic_slice_in_dim(gain, at, piece, 0),
        )

    pieces = steps * CHUNKS

    def outgoing(number, carried):
        number = jnp.clip(number, 0, pieces - 1)
        mine = owners[number // CHUNKS] // 2 == chip
        return own(number) if carried is None else jnp.where(mine, own(number), carried)

    rose, fell = [], []
    for turn in range(pieces + chips - 2):
        rising = outgoing(turn - chip, rose[-1] if rose else None)
        falling = outgoing(turn - (chips - 1 - chip), fell[-1] if fell else None)
        rose.append(lax.ppermute(rising, "long", up))
        fell.append(lax.ppermute(falling, "long", down))

    results = []
    most = 0
    for step in range(steps):
        source = owners[step] // 2
        kept = []
        for number in range(step * CHUNKS, (step + 1) * CHUNKS):
            value = own(number)
            for place in range(chips):
                if place > 0:
                    below = (chip == place) & (source < chip)
                    value = jnp.where(below, rose[number + place - 1], value)
                if place < chips - 1:
                    above = (chip == place) & (source > chip)
                    value = jnp.where(above, fell[number + chips - 2 - place], value)
            kept.append(value)
        start = half - (CHUNKS - 1) * piece
        pattern = kept[-1][start : start + amp_pattern.shape[0], : amp_pattern.shape[1]]
        here, count = by_parity(pattern.astype(jnp.int32))
        most = jnp.maximum(most, jnp.max(jnp.sum(here, axis=-1)))
        rank = jnp.maximum(count - 1, 0)
        near = (rank // (slots // 2)) == core
        at = rank % (slots // 2) * TILE + jnp.where(near, 0, share)
        ranks = jnp.where((here > 0) & (rank < slots), at, 2 * share).astype(jnp.int32)
        other = [lax.ppermute(value, "long", swap) for value in kept]
        nothing = jnp.zeros((TILE, LANES), amplitudes.dtype)
        panel = jnp.concatenate(kept + other + [nothing], 0)
        partial_value = multiply(panel, ranks, sparse_int, rows)
        total = lax.psum_scatter(partial_value, "grp", scatter_dimension=1, tiled=True)
        results.append(total.astype(amplitudes.dtype))
    quick = jnp.stack(results, 0)

    over = lax.psum((most > slots).astype(jnp.float32), "grp")
    return lax.cond(
        over > 0,
        lambda: dense_path(amplitudes, sparse_int, amp_pattern, owners),
        lambda: quick,
    )


def solution(mesh):
    placed = (P("long", "grp"), P("grp", "long"), P("long", "grp"), P("grp", "long"), P())
    return jax.shard_map(
        functools.partial(per_device, mesh.shape["long"], mesh.shape["grp"]),
        mesh=mesh,
        in_specs=placed,
        out_specs=P(None, None, ("long", "grp")),
        check_vma=False,
    )
```
